32 devices in a mesh: section: 2 (over core), seq: 4 (over z), head: 4 (over y, x).
Axes of the slice: x: 2, y: 2, z: 4, core: 2. Of those that a mesh axis runs over, the one named last changes fastest.
Arguments:
- inputs: bfloat16 [2, 2048, 1024], P(None, 'seq'), may hold values from -6 to 6
- positions: int32 [2, 2048], P(None, 'seq'), may hold values from 0 to 1535, as said below
- cotangent: bfloat16 [2, 2048, 1024], P(None, 'seq'), may hold values from -6 to 6
- qkv_weight: bfloat16 [2, 1024, 3, 1024], P('section', 'seq', None, 'head'), may hold values from -0.1875 to 0.1875
- out_weight: bfloat16 [2, 1024, 1024], P('section', 'seq', 'head'), may hold values from -1.5 to 1.5
- gate_up_weight: bfloat16 [2, 1024, 2, 2816], P('section', 'seq', None, 'head'), may hold values from -0.1875 to 0.1875
- down_weight: bfloat16 [2, 1024, 2816], P('section', 'seq', 'head'), may hold values from -0.109375 to 0.109375
- attn_gain: bfloat16 [2, 1024], P('section', 'seq'), may hold values from 0.5 to 1.5
- ffn_gain: bfloat16 [2, 1024], P('section', 'seq'), may hold values from 0.5 to 1.5
Outputs:
- activations: bfloat16 [2, 2, 2048, 1024], P('section', None, 'seq')
- input_grads: float32 [2, 2, 2048, 1024], P('section', None, 'seq')
- qkv_grad: float32 [2, 1024, 3, 1024], P('section', 'seq', None, 'head')
- out_grad: float32 [2, 1024, 1024], P('section', 'seq', 'head')
- gate_up_grad: float32 [2, 1024, 2, 2816], P('section', 'seq', None, 'head')
- down_grad: float32 [2, 1024, 2816], P('section', 'seq', 'head')
- attn_gain_grad: float32 [2, 1024], P('section', 'seq')
- ffn_gain_grad: float32 [2, 1024], P('section', 'seq')
The draws below stay inside these ranges and needn't reach their ends.
Inputs may be any that keep to these rules, and one draw needn't show every extreme that they name: Each micro-batch is packed with documents laid end to end: a first document of 1 to 511 tokens, then one document of exactly 1536 tokens, then one or two documents that fill the rest; a token's position is its offset in its document, so positions rise by one inside a document and restart at 0 where the next begins.
All inputs are finite; a program needn't handle non-finite values.
Results may differ from the reference program's by a relative error of at most 0.03.
Values may be sent and summed in bfloat16 or wider, within the bound.
No kernel may reach another device: no remote copies, remote signals or barrier semaphores. Data moves between devices by JAX's collectives and lax.ppermute only.
A program may use at most 256 MiB of HBM per device.

```python
import jax
import jax.numpy as jnp
from jax import lax

D = 1024
HEADS = 16
HEAD_DIM = 64
FF = 2816
MB = 2
TOK_DEV = 512
TOKENS = 2048
DOC = 1536
N_SECTION = 2


def draw_positions(key, part):

    def one(sub):
        first_key, second_key = jax.random.split(sub)
        lead = jax.random.randint(first_key, (), 1, TOK_DEV).astype(jnp.int32)
        rest = (TOK_DEV - lead).astype(jnp.int32)
        cut = (1 + jax.random.randint(second_key, (), 0, 1 << 20) % rest).astype(jnp.int32)
        index = jnp.arange(TOKENS, dtype=jnp.int32)
        after = index - lead - DOC
        tail = jnp.where(after < cut, after, after - cut)
        middle = index - lead
        return jnp.where(index < lead, index, jnp.where(after < 0, middle, tail)).astype(jnp.int32)
    return jax.vmap(one)(jax.random.split(key, MB))


def strengthened(entries, own_key, source, target, blocks, factor):
    owner, partner = [(jnp.arange(entries.shape[axis_at]) // (entries.shape[axis_at] // blocks)).reshape([-1 if axis == axis_at else 1 for axis in range(entries.ndim)]) for axis_at in (source, target)]
    chosen = jax.random.permutation(own_key, blocks)[partner]
    strong = (owner == chosen) | (owner == (partner + blocks // 2) % blocks)
    return jnp.where(strong, factor * entries, entries)


def block_scale(own_key, shape, cuts, least, largest):
    loudness = 1.0
    for dim, shards_of in cuts:
        heights = jax.random.uniform(jax.random.fold_in(jax.random.fold_in(own_key, 6), dim), (shards_of,), jnp.float32, least / len(cuts), largest / len(cuts))
        loudness = loudness * jnp.repeat(jnp.exp(heights), shape[dim] // shards_of).reshape((-1,) + (1,) * (len(shape) - 1 - dim))
    return loudness


def noise(rng, dims, scale, bound, cuts=(), held_as=jnp.bfloat16):
    entries = scale * jax.random.normal(rng, dims, jnp.float32)
    if cuts:
        entries = entries * block_scale(rng, dims, cuts, -0.22, 0.18)
    return jnp.clip(entries, -bound, bound).astype(held_as)


def bell_draw_with(stream_key, dims, spread, reach, pieces, heavy, kind=jnp.bfloat16):
    drawn = spread * jax.random.normal(stream_key, dims, jnp.float32)
    if pieces:
        drawn = drawn * block_scale(stream_key, dims, pieces, -0.22, 0.18)
    return jnp.clip(strengthened(drawn, jax.random.fold_in(stream_key, 3), *heavy), -reach, reach).astype(kind)


def setup_inputs(seed: int = 0) -> dict:
    key_of = jax.random.split(jax.random.key(seed), 10)
    inputs = bell_draw_with(key_of[0], (MB, TOKENS, D), 1.0, 6.0, ((1, 4),), (1, 2, 4, 2.0))
    positions = draw_positions(jax.random.fold_in(key_of[9], 71), 0)
    cotangent = bell_draw_with(key_of[2], (MB, TOKENS, D), 1.0, 6.0, ((1, 4),), (1, 2, 4, 2.0))
    qkv_weight = noise(key_of[3], (N_SECTION, D, 3, D), D ** -0.5, 0.1875, ((0, 2), (1, 4), (3, 4)))
    out_weight = noise(key_of[4], (N_SECTION, D, D), HEADS ** -0.5, 1.5, ((0, 2), (1, 4), (2, 4)))
    gate_up_weight = noise(key_of[5], (N_SECTION, D, 2, FF), D ** -0.5, 0.1875, ((0, 2), (1, 4), (3, 4)))
    down_weight = noise(key_of[6], (N_SECTION, D, FF), FF ** -0.5, 0.109375, ((0, 2), (1, 4), (2, 4)))
    attn_gain = jnp.clip(1.0 + 0.1 * jax.random.normal(key_of[7], (N_SECTION, D), jnp.float32), 0.5, 1.5).astype(jnp.bfloat16)
    ffn_gain = jnp.clip(1.0 + 0.1 * jax.random.normal(key_of[8], (N_SECTION, D), jnp.float32), 0.5, 1.5).astype(jnp.bfloat16)
    return dict(inputs=inputs, positions=positions, cotangent=cotangent, qkv_weight=qkv_weight, out_weight=out_weight, gate_up_weight=gate_up_weight, down_weight=down_weight, attn_gain=attn_gain, ffn_gain=ffn_gain)


@jax.custom_vjp
def low(v):
    return lax.optimization_barrier(v.astype(jnp.bfloat16)).astype(jnp.float32)

@jax.custom_vjp
def low_back(v):
    return v

def low_keep(v):
    return (low(v), None)

def low_pass(kept, grad):
    return (grad,)

def back_keep(v):
    return (v, None)

def back_low(kept, grad):
    return (low(grad),)
low.defvjp(low_keep, low_pass)
low_back.defvjp(back_keep, back_low)

def angles(positions):
    half = HEAD_DIM // 2
    rates = 10000.0 ** (-jnp.arange(half, dtype=jnp.float32) / half)
    turned = positions.astype(jnp.float32)[:, None] * rates[None, :]
    return (jnp.cos(turned)[:, None, :], jnp.sin(turned)[:, None, :])

def rotate(vectors, cosine, sine):
    half = HEAD_DIM // 2
    first = vectors[..., :half]
    second = vectors[..., half:]
    return jnp.concatenate([first * cosine - second * sine, second * cosine + first * sine], axis=-1)

def rms_norm(values, gain):
    return values * lax.rsqrt(lax.optimization_barrier(jnp.mean(values * values, axis=-1, keepdims=True)) + 1e-06) * gain

def attend(queries, keys, values, positions):
    total = queries.shape[0]
    block = min(512, total)
    front = jnp.zeros((DOC,) + keys.shape[1:], jnp.float32)
    keys_padded = jnp.concatenate([front, keys], axis=0)
    values_padded = jnp.concatenate([front, values], axis=0)
    scale = HEAD_DIM ** (-0.5)

    def one_block(start):
        query_rows = lax.dynamic_slice_in_dim(queries, start, block, 0)
        key_rows = lax.dynamic_slice_in_dim(keys_padded, start, DOC + block, 0)
        value_rows = lax.dynamic_slice_in_dim(values_padded, start, DOC + block, 0)
        offsets = lax.dynamic_slice_in_dim(positions, start, block, 0)
        query_index = start + jnp.arange(block, dtype=jnp.int32)
        key_index = start - DOC + jnp.arange(DOC + block, dtype=jnp.int32)
        allowed = (key_index[None, :] <= query_index[:, None]) & (key_index[None, :] >= (query_index - offsets)[:, None])
        scores = low_back(jnp.einsum('qhd,khd->hqk', query_rows, key_rows, precision=lax.Precision.HIGHEST) * scale)
        scores = jnp.where(allowed[None], scores, -1e+30)
        weights = low(jax.nn.softmax(scores, axis=-1))
        return jnp.einsum('hqk,khd->qhd', weights, value_rows, precision=lax.Precision.HIGHEST)
    starts = jnp.arange(total // block, dtype=jnp.int32) * block
    return lax.map(jax.checkpoint(one_block), starts).reshape(queries.shape)

def layer(inputs, positions, weights, first_values):
    w_project, w_out, w_gate_up, w_down, gain_attn, gain_ffn = weights
    count = inputs.shape[0]
    shape = (count, HEADS, HEAD_DIM)
    normed = low(rms_norm(inputs, gain_attn))
    project = jnp.einsum('td,dce->tce', normed, w_project, precision=lax.Precision.HIGHEST)
    cosine, sine = angles(positions)
    queries = low(rotate(low_back(project[:, 0]).reshape(shape), cosine, sine))
    keys = low(rotate(low_back(project[:, 1]).reshape(shape), cosine, sine))
    raw_values = low_back(project[:, 2])
    if first_values is None:
        values = low(raw_values)
    else:
        values = low(0.5 * raw_values + 0.5 * low_back(first_values))
    attended = low(low_back(attend(queries, keys, values.reshape(shape), positions).reshape(count, HEADS * HEAD_DIM)))
    hidden = inputs + low_back(jnp.einsum('ti,oi->to', attended, w_out, precision=lax.Precision.HIGHEST))
    normed_ffn = low(rms_norm(hidden, gain_ffn))
    gate_up = jnp.einsum('td,dcf->tcf', normed_ffn, w_gate_up, precision=lax.Precision.HIGHEST)
    gate = low_back(gate_up[:, 0])
    upward = low_back(gate_up[:, 1])
    active = low(jax.nn.silu(gate) * upward)
    output = hidden + low_back(jnp.einsum('tf,df->td', active, w_down, precision=lax.Precision.HIGHEST))
    return (output, values)

def forward(inputs, probe, first_layer, second_layer, positions):

    def one(carry, item):
        rows, extra, offsets = item
        middle_out, first_values = layer(rows, offsets, first_layer, None)
        middle = low(low_back(middle_out)) + extra
        final, unused = layer(middle, offsets, second_layer, first_values)
        return (carry, (final, middle))
    carry, (final, middle) = lax.scan(one, jnp.zeros((), jnp.float32), (inputs, probe, positions))
    return (final, middle)

def reference(inputs, positions, cotangent, qkv_weight, out_weight, gate_up_weight, down_weight, attn_gain, ffn_gain):
    weights = [weight.astype(jnp.float32) for weight in (qkv_weight, out_weight, gate_up_weight, down_weight, attn_gain, ffn_gain)]
    first_layer = tuple((weight[0] for weight in weights))
    second_layer = tuple((weight[1] for weight in weights))
    start = inputs.astype(jnp.float32)
    probe = jnp.zeros_like(start)

    def whole(start_rows, probe_rows, first_weights, second_weights):
        return forward(start_rows, probe_rows, first_weights, second_weights, positions)
    final, pullback, middle = jax.vjp(whole, start, probe, first_layer, second_layer, has_aux=True)
    grad_input, grad_middle, grad_first, grad_second = pullback(cotangent.astype(jnp.float32))
    activations = jnp.stack([middle, final]).astype(jnp.bfloat16)
    input_grads = jnp.stack([grad_input, grad_middle])
    grads = [jnp.stack([first, second]) for first, second in zip(grad_first, grad_second)]
    return (activations, input_grads, grads[0], grads[1], grads[2], grads[3], grads[4], grads[5])
```

```python
import jax
import jax.numpy as jnp
from jax import lax
from jax.experimental import pallas as pl
from jax.experimental.pallas import tpu as pltpu
from jax.sharding import PartitionSpec as P

HEAD_DIM = 64
HALF = HEAD_DIM // 2
EPS = 1e-06
MASKED = -1e30
SCALE = HEAD_DIM ** (-0.5)
BF16 = jnp.bfloat16
F32 = jnp.float32


def dot(a, b, dims):
    return lax.dot_general(a, b, (dims, ((), ())), preferred_element_type=F32)


def head_peer(x, k):
    n = lax.axis_size("head")
    return lax.ppermute(x, "head", [(i, i ^ k) for i in range(n)])


def seq_shift(x, k):
    n = lax.axis_size("seq")
    return lax.ppermute(x, "seq", [(i, (i + k) % n) for i in range(n)])


def core_swap(x):
    return lax.ppermute(x, "section", [(0, 1), (1, 0)])


def reduce_tokens(partial_sum):
    n = lax.axis_size("head")
    part = partial_sum.shape[0] // n
    low = partial_sum.astype(BF16)
    total = partial_sum[:part]
    for k in range(1, n):
        total = total + head_peer(low[k * part : (k + 1) * part], k).astype(F32)
    return total


def gather_tokens(own):
    n = lax.axis_size("head")
    return jnp.concatenate([own] + [head_peer(own, k) for k in range(1, n)], axis=0)


def peer_order(x):
    n = lax.axis_size("head")
    me = lax.axis_index("head")
    part = x.shape[0] // n
    return jnp.concatenate(
        [lax.dynamic_slice_in_dim(x, (me ^ k) * part, part, 0) for k in range(n)], axis=0
    )


def seq_slots(x):
    n = lax.axis_size("seq")
    return jnp.stack([x] + [seq_shift(x, k) for k in range(1, n)], axis=0)


def to_heads(x):
    n = lax.axis_size("seq")
    me = lax.axis_index("seq")

    def block(k):
        return lax.dynamic_index_in_dim(x, (me + k) % n, 0, keepdims=False)

    return jnp.stack([block(0)] + [seq_shift(block(k), k) for k in range(1, n)], axis=0)


def to_tokens(x):
    n = lax.axis_size("seq")
    me = lax.axis_index("seq")
    parts = jnp.stack([x[0]] + [seq_shift(x[k], -k) for k in range(1, n)], axis=0)
    return jnp.stack(
        [lax.dynamic_index_in_dim(parts, (h - me) % n, 0, keepdims=False) for h in range(n)],
        axis=0,
    )


def visible(block, xor, lo_token, queries, size):
    rows = lax.broadcasted_iota(jnp.int32, (size, 1), 0)
    keys = block * size + (rows ^ xor)
    return (keys <= queries) & (keys >= lo_token)


def attend_kernel(lo, qslot, kslot, base, q_ref, k_ref, v_ref, pos_ref, o_ref, ob_ref, lse_ref, kt_ref):
    i = pl.program_id(1)
    size = q_ref.shape[-1]
    blocks = k_ref.shape[1]

    @pl.when(i == 0)
    def _():
        for j in range(blocks):
            kt_ref[j] = jnp.transpose(k_ref[0, j, 0])

    xor = base[1]
    here = base[0] + i
    query = (q_ref[0, 0, 0].astype(F32) * SCALE).astype(BF16)
    lanes = lax.broadcasted_iota(jnp.int32, (1, size), 1)
    index = here * size + (lanes ^ xor)
    first = index - pos_ref[0]

    def step(j, carry):
        peak, total, acc = carry
        slot = kslot[j]
        s = dot(kt_ref[slot], query, ((1,), (0,)))
        s = jnp.where(visible(j, xor, first, index, size), s, MASKED)
        fresh = jnp.maximum(peak, jnp.max(s, axis=0, keepdims=True))
        p = jnp.exp(s - fresh)
        shrink = jnp.exp(peak - fresh)
        total = total * shrink + jnp.sum(p, axis=0, keepdims=True)
        acc = acc * shrink + dot(v_ref[0, slot, 0], p.astype(BF16), ((1,), (0,)))
        return fresh, total, acc

    peak, total, acc = lax.fori_loop(
        lo[i],
        here + 1,
        step,
        (
            jnp.full((1, size), MASKED, F32),
            jnp.zeros((1, size), F32),
            jnp.zeros((HEAD_DIM, size), F32),
        ),
    )
    out = acc / total
    o_ref[0, 0] = out
    ob_ref[0, 0] = out.astype(BF16)
    lse_ref[0, 0] = peak + jnp.log(total)


def grad_kernel(
    lo, qslot, kslot, base,
    q_ref, k_ref, v_ref, pos_ref, o_ref, dob_ref, lse_ref,
    dq_ref, dk_ref, dv_ref, kt_ref, vt_ref,
):
    i = pl.program_id(1)
    size = q_ref.shape[-1]
    blocks = k_ref.shape[1]

    @pl.when(i == 0)
    def _():
        for j in range(blocks):
            kt_ref[j] = jnp.transpose(k_ref[0, j, 0])
            vt_ref[j] = jnp.transpose(v_ref[0, j, 0])
        dk_ref[...] = jnp.zeros_like(dk_ref)
        dv_ref[...] = jnp.zeros_like(dv_ref)

    xor = base[1]
    here = base[0] + i
    query = (q_ref[0, 0, 0].astype(F32) * SCALE).astype(BF16)
    dob = dob_ref[0, 0]
    lse = lse_ref[0, 0]
    delta = jnp.sum(dob.astype(F32) * o_ref[0, 0], axis=0, keepdims=True)
    lanes = lax.broadcasted_iota(jnp.int32, (1, size), 1)
    index = here * size + (lanes ^ xor)
    first = index - pos_ref[0]

    def step(j, dq):
        slot = kslot[j]
        s = dot(kt_ref[slot], query, ((1,), (0,)))
        p = jnp.where(visible(j, xor, first, index, size), jnp.exp(s - lse), 0.0)
        dp = dot(vt_ref[slot], dob, ((1,), (0,)))
        ds = (p * (dp - delta)).astype(BF16)
        dv_ref[0, slot] += dot(dob, p.astype(BF16), ((1,), (1,)))
        dk_ref[0, slot] += dot(query, ds, ((1,), (1,)))
        return dq + dot(k_ref[0, slot, 0], ds, ((1,), (0,)))

    dq = lax.fori_loop(lo[i], here + 1, step, jnp.zeros((HEAD_DIM, size), F32))
    dq_ref[0, 0] = dq * SCALE


def attention_specs(heads, queries, keys, size):
    def q_at(h, i, lo, qslot, kslot, base):
        return (h, qslot[i], 0, 0, 0)

    def k_at(h, i, *_):
        return (h, 0, 1, 0, 0)

    def v_at(h, i, *_):
        return (h, 0, 2, 0, 0)

    def row_at(h, i, lo, qslot, kslot, base):
        return (qslot[i], 0, 0)

    def own_at(h, i, lo, qslot, kslot, base):
        return (h, qslot[i], 0, 0)

    q_spec = pl.BlockSpec((1, 1, 1, HEAD_DIM, size), q_at)
    k_spec = pl.BlockSpec((1, keys, 1, HEAD_DIM, size), k_at)
    v_spec = pl.BlockSpec((1, keys, 1, HEAD_DIM, size), v_at)
    pos_spec = pl.BlockSpec((1, 1, size), row_at)
    wide = pl.BlockSpec((1, 1, HEAD_DIM, size), own_at)
    thin = pl.BlockSpec((1, 1, 1, size), own_at)
    full = pl.BlockSpec((1, keys, HEAD_DIM, size), lambda h, i, *_: (h, 0, 0, 0))
    return q_spec, k_spec, v_spec, pos_spec, wide, thin, full


def attend(scalars, q, kv, pos):
    heads, queries, _, _, size = q.shape
    keys = kv.shape[1]
    q_spec, k_spec, v_spec, pos_spec, wide, thin, full = attention_specs(heads, queries, keys, size)
    pairs = heads * queries * keys * size * size
    return pl.pallas_call(
        attend_kernel,
        grid_spec=pltpu.PrefetchScalarGridSpec(
            num_scalar_prefetch=4,
            grid=(heads, queries),
            in_specs=[q_spec, k_spec, v_spec, pos_spec],
            out_specs=[wide, wide, thin],
            scratch_shapes=[pltpu.VMEM((keys, size, HEAD_DIM), BF16)],
        ),
        out_shape=[
            jax.ShapeDtypeStruct((heads, queries, HEAD_DIM, size), F32),
            jax.ShapeDtypeStruct((heads, queries, HEAD_DIM, size), BF16),
            jax.ShapeDtypeStruct((heads, queries, 1, size), F32),
        ],
        compiler_params=pltpu.CompilerParams(vmem_limit_bytes=40 << 20),
        cost_estimate=pl.CostEstimate(
            flops=4 * pairs * HEAD_DIM, bytes_accessed=4 * q.size, transcendentals=pairs
        ),
        name="attend",
    )(*scalars, q, kv, kv, pos)


def attend_grad(scalars, q, kv, pos, o, dob, lse):
    heads, queries, _, _, size = q.shape
    keys = kv.shape[1]
    q_spec, k_spec, v_spec, pos_spec, wide, thin, full = attention_specs(heads, queries, keys, size)
    pairs = heads * queries * keys * size * size
    return pl.pallas_call(
        grad_kernel,
        grid_spec=pltpu.PrefetchScalarGridSpec(
            num_scalar_prefetch=4,
            grid=(heads, queries),
            in_specs=[q_spec, k_spec, v_spec, pos_spec, wide, wide, thin],
            out_specs=[wide, full, full],
            scratch_shapes=[pltpu.VMEM((keys, size, HEAD_DIM), BF16)] * 2,
        ),
        out_shape=[
            jax.ShapeDtypeStruct((heads, queries, HEAD_DIM, size), F32),
            jax.ShapeDtypeStruct((heads, keys, HEAD_DIM, size), F32),
            jax.ShapeDtypeStruct((heads, keys, HEAD_DIM, size), F32),
        ],
        compiler_params=pltpu.CompilerParams(vmem_limit_bytes=48 << 20),
        cost_estimate=pl.CostEstimate(
            flops=10 * pairs * HEAD_DIM, bytes_accessed=8 * q.size, transcendentals=pairs
        ),
        name="attend_grad",
    )(*scalars, q, kv, kv, pos, o, dob, lse)


def turn(w, cosine, sine):
    first, second = w[..., :HALF, :], w[..., HALF:, :]
    return jnp.concatenate(
        [first * cosine - second * sine, second * cosine + first * sine], axis=-2
    )


def turn_back(w, cosine, sine):
    first, second = w[..., :HALF, :], w[..., HALF:, :]
    return jnp.concatenate(
        [first * cosine + second * sine, second * cosine - first * sine], axis=-2
    )


def gather_layers(shard):
    core = lax.axis_index("section")
    half = shard.shape[0] // 2
    mine = lax.dynamic_slice_in_dim(shard, core * half, half, 0)
    got = core_swap(lax.dynamic_slice_in_dim(shard, (1 - core) * half, half, 0))
    halves = (jnp.where(core == 0, mine, got), jnp.where(core == 0, got, mine))
    return [lax.all_gather(h, ("seq", "section"), axis=0, tiled=True) for h in halves]


def on_device(
    inputs, positions, cotangent, qkv_weight, out_weight, gate_up_weight, down_weight,
    attn_gain, ffn_gain,
):
    core = lax.axis_index("section")
    seq = lax.axis_index("seq")
    devices = lax.axis_size("seq")
    peers = lax.axis_size("head")
    _, rows, width = inputs.shape
    part = rows // peers
    heads = qkv_weight.shape[3] // HEAD_DIM
    local = heads * HEAD_DIM
    hidden = down_weight.shape[2]
    by_head = devices == heads

    own = width // devices
    w_qkv = gather_layers(
        qkv_weight[0].reshape(own, 3, heads, HEAD_DIM).transpose(0, 2, 1, 3).reshape(own, 3 * local)
    )
    w_out = gather_layers(out_weight[0])
    w_gate_up = gather_layers(gate_up_weight[0].reshape(own, 2 * hidden))
    w_down = gather_layers(down_weight[0])
    gain = jnp.stack([attn_gain[0], ffn_gain[0]])
    gain_other = core_swap(gain)
    gain = jnp.where(core == 0, jnp.stack([gain, gain_other]), jnp.stack([gain_other, gain]))
    gain = seq_slots(gain)
    gain = jnp.stack(
        [
            lax.dynamic_index_in_dim(gain, (seq - j) % devices, 0, keepdims=False)
            for j in range(devices)
        ],
        axis=2,
    ).reshape(2, 2, width)
    gain = gain.astype(F32)

    x0 = peer_order(lax.dynamic_index_in_dim(inputs, core, 0, keepdims=False))
    gy1 = peer_order(lax.dynamic_index_in_dim(cotangent, core, 0, keepdims=False))
    pos = peer_order(lax.dynamic_index_in_dim(positions, core, 0, keepdims=False))
    pos = seq_slots(pos)
    xor = lax.axis_index("head") * part
    slots = (seq - jnp.arange(devices, dtype=jnp.int32)) % devices
    token = slots[:, None] * rows + (jnp.arange(rows, dtype=jnp.int32) ^ xor)[None, :]
    lowest = jnp.min(token - pos, axis=1) // rows
    rates = 10000.0 ** (-jnp.arange(HALF, dtype=F32) / HALF)
    theta = pos.astype(F32)[:, None, :] * rates[None, :, None]
    cosine, sine = jnp.cos(theta), jnp.sin(theta)
    own_cos, own_sin = cosine[0], sine[0]
    if by_head:
        scalars = (
            lowest[slots],
            slots,
            slots,
            jnp.stack([jnp.zeros((), jnp.int32), xor]),
        )
        pos_rows = pos[:, None, :]
        back_cos, back_sin = cosine, sine
    else:
        scalars = (
            lowest[:1],
            jnp.zeros((1,), jnp.int32),
            jnp.arange(devices, dtype=jnp.int32),
            jnp.stack([seq, xor]),
        )
        pos_rows = pos[:1, None, :]
        back_cos, back_sin = own_cos, own_sin

    def norm(v, g):
        inverse = lax.rsqrt(jnp.mean(v * v, axis=-1, keepdims=True) + EPS)
        return inverse, (v * inverse * g).astype(BF16)

    def forward(layer, x, first_value):
        x_full = x.astype(F32)
        _, n1 = norm(x_full, gain[layer, 0])
        p = dot(w_qkv[layer], n1, ((0,), (1,))).reshape(heads, 3, HEAD_DIM, rows)
        q = turn(p[:, 0], own_cos, own_sin).astype(BF16)
        k = turn(p[:, 1], own_cos, own_sin).astype(BF16)
        v = p[:, 2]
        if first_value is not None:
            v = 0.5 * v + 0.5 * first_value.astype(F32)
        v = v.astype(BF16)
        packed = jnp.stack([q, k, v], axis=1)
        if by_head:
            query = to_heads(packed)[None]
            key_value = query
        else:
            query = packed[:, None]
            key_value = jnp.transpose(lax.all_gather(packed, "seq"), (1, 0, 2, 3, 4))
        o, ob, lse = attend(scalars, query, key_value, pos_rows)
        ob = (to_tokens(ob[0]) if by_head else ob[:, 0]).reshape(local, rows)
        x_own = x_full[:part]
        hid = x_own + reduce_tokens(dot(ob, w_out[layer], ((0,), (1,))))
        r2, n2_own = norm(hid, gain[layer, 1])
        n2 = gather_tokens(n2_own)
        gate_up = dot(n2, w_gate_up[layer], ((1,), (0,)))
        gate, up = gate_up[:, :hidden], gate_up[:, hidden:]
        act = (jax.nn.silu(gate) * up).astype(BF16)
        y_own = hid + reduce_tokens(dot(act, w_down[layer], ((1,), (1,))))
        y = gather_tokens(y_own.astype(BF16))
        kept = (x_own, n1, query, key_value, o, lse, ob, hid, r2, n2, gate, up, act)
        return y, v, kept

    def backward(layer, gyb, gfirst, kept):
        x_own, n1, query, key_value, o, lse, ob, hid, r2, n2, gate, up, act = kept
        sigmoid = jax.nn.sigmoid(gate)
        da = dot(gyb, w_down[layer], ((1,), (0,)))
        dgate = da * up * sigmoid * (1.0 + gate * (1.0 - sigmoid))
        dup = da * (gate * sigmoid)
        dgu = jnp.concatenate([dgate, dup], axis=1).astype(BF16)
        dn2 = reduce_tokens(dot(dgu, w_gate_up[layer], ((1,), (1,))))
        g_down = dot(gyb, act, ((0,), (0,))).astype(BF16)
        g_gate_up = dot(n2, dgu, ((0,), (0,))).astype(BF16)
        c2 = hid * r2
        g_ffn_gain = jnp.sum(dn2 * c2, axis=0)
        e2 = dn2 * gain[layer, 1]
        gh = gyb[:part].astype(F32) + r2 * (e2 - c2 * jnp.mean(e2 * c2, axis=-1, keepdims=True))
        ghb = gather_tokens(gh.astype(BF16))
        g_out = dot(ghb, ob, ((0,), (1,))).astype(BF16)
        dob = dot(w_out[layer], ghb, ((0,), (1,))).astype(BF16).reshape(heads, HEAD_DIM, rows)
        dob = to_heads(dob)[None] if by_head else dob[:, None]
        dq, dk, dv = attend_grad(scalars, query, key_value, pos_rows, o, dob, lse)
        if by_head:
            dq, dk, dv = dq[0], dk[0], dv[0]
        else:
            dq = dq[:, 0]
            dkv = jnp.stack([dk, dv], axis=1).transpose(2, 0, 1, 3, 4).astype(BF16)
            dkv = lax.psum_scatter(dkv, "seq", scatter_dimension=0, tiled=False).astype(F32)
            dk, dv = dkv[:, 0], dkv[:, 1]
        dq = turn_back(dq, back_cos, back_sin).astype(BF16)
        dk = turn_back(dk, back_cos, back_sin).astype(BF16)
        if gfirst is None:
            dv = (0.5 * dv).astype(BF16)
        else:
            dv = (dv + gfirst.astype(F32)).astype(BF16)
        packed = jnp.stack([dq, dk, dv], axis=1)
        if by_head:
            packed = to_tokens(packed)
        dqkv = packed.reshape(3 * local, rows)
        dn1 = reduce_tokens(dot(dqkv, w_qkv[layer], ((0,), (1,))))
        g_qkv = dot(n1, dqkv, ((0,), (1,))).astype(BF16)
        r1 = lax.rsqrt(jnp.mean(x_own * x_own, axis=-1, keepdims=True) + EPS)
        c1 = x_own * r1
        g_attn_gain = jnp.sum(dn1 * c1, axis=0)
        e1 = dn1 * gain[layer, 0]
        gx = gh + r1 * (e1 - c1 * jnp.mean(e1 * c1, axis=-1, keepdims=True))
        gx = gather_tokens(gx.astype(BF16))
        scattered = [
            lax.psum_scatter(g, ("seq", "section"), scatter_dimension=0, tiled=True)
            for g in (g_down, g_gate_up, g_out, g_qkv)
        ]
        return gx, dv, scattered, jnp.stack([g_attn_gain, g_ffn_gain])

    y0, v0, kept0 = forward(0, x0, None)
    y1, _, kept1 = forward(1, y0, v0)
    gx1, gfirst, grads1, gains1 = backward(1, gy1, None, kept1)
    gx0, _, grads0, gains0 = backward(0, gx1, gfirst, kept0)

    def place(first_layer, second_layer):
        other_first = lax.ppermute(first_layer, "section", [(1, 0)])
        other_second = lax.ppermute(second_layer, "section", [(0, 1)])
        return (
            jnp.where(core == 0, first_layer, other_second),
            jnp.where(core == 0, other_first, second_layer),
        )

    def place_tokens(first_layer, second_layer, dtype):
        pair = place(first_layer, second_layer)
        return jnp.stack([peer_order(m).astype(dtype) for m in pair])[None]

    def place_rows(first_layer, second_layer):
        pair = place(first_layer, second_layer)
        return jnp.concatenate(pair, axis=0).astype(F32)[None]

    activations = place_tokens(y0, y1, BF16)
    input_grads = place_tokens(gx0, gx1, F32)
    down_grad, gate_up_grad, out_grad, qkv_grad = [
        place_rows(a, b) for a, b in zip(grads0, grads1)
    ]
    qkv_grad = (
        qkv_grad.reshape(1, own, heads, 3, HEAD_DIM)
        .transpose(0, 1, 3, 2, 4)
        .reshape(1, own, 3, local)
    )
    gate_up_grad = gate_up_grad.reshape(1, own, 2, hidden)
    gains = jnp.stack([gains0, gains1])
    for axis, count in (("section", 2), ("head", peers), ("seq", devices)):
        k = 1
        while k < count:
            gains = gains + lax.ppermute(gains, axis, [(i, i ^ k) for i in range(count)])
            k *= 2
    gains = lax.dynamic_index_in_dim(gains, core, 0, keepdims=False)
    gains = lax.dynamic_slice_in_dim(gains, seq * own, own, 1)
    return (
        activations,
        input_grads,
        qkv_grad,
        out_grad,
        gate_up_grad,
        down_grad,
        gains[0][None],
        gains[1][None],
    )


def solution(mesh):
    placed = (
        P(None, "seq", None),
        P(None, "seq"),
        P(None, "seq", None),
        P("section", "seq", None, "head"),
        P("section", "seq", "head"),
        P("section", "seq", None, "head"),
        P("section", "seq", "head"),
        P("section", "seq"),
        P("section", "seq"),
    )
    return jax.shard_map(
        on_device,
        mesh=mesh,
        in_specs=placed,
        out_specs=(
            P("section", None, "seq", None),
            P("section", None, "seq", None),
            P("section", "seq", None, "head"),
            P("section", "seq", "head"),
            P("section", "seq", None, "head"),
            P("section", "seq", "head"),
            P("section", "seq"),
            P("section", "seq"),
        ),
        check_vma=False,
    )
```

```python
import jax
import jax.numpy as jnp
from jax import lax
from jax.experimental import pallas as pl
from jax.experimental.layout import Layout, with_layout_constraint
from jax.experimental.pallas import tpu as pltpu
from jax.sharding import PartitionSpec as P

HEAD_DIM = 64
HALF = HEAD_DIM // 2
EPS = 1e-06
MASKED = -1e30
SCALE = HEAD_DIM ** (-0.5)
BF16 = jnp.bfloat16
F32 = jnp.float32


def dot(a, b, dims):
    return lax.dot_general(a, b, (dims, ((), ())), preferred_element_type=F32)


def head_peer(x, k):
    n = lax.axis_size("head")
    return lax.ppermute(x, "head", [(i, i ^ k) for i in range(n)])


def seq_shift(x, k):
    n = lax.axis_size("seq")
    return lax.ppermute(x, "seq", [(i, (i + k) % n) for i in range(n)])


def core_swap(x):
    return lax.ppermute(x, "section", [(0, 1), (1, 0)])


barrier = lax.optimization_barrier


def beside(exchange, value, work, operands):
    value, operands = barrier((value, operands))
    got = exchange(value)
    done = work(*operands)
    return barrier((got, done))


def reduce_tokens(partial_sum, work=None, operands=()):
    n = lax.axis_size("head")
    part = partial_sum.shape[0] // n

    def exchange(low):
        return [head_peer(low[k * part : (k + 1) * part], k) for k in range(1, n)]

    low = partial_sum.astype(BF16)
    if work is None:
        got = exchange(low)
    else:
        got, done = beside(exchange, low, work, operands)
    total = low[:part].astype(F32)
    for g in got:
        total = total + g.astype(F32)
    return total if work is None else (total, done)


def gather_tokens(own, work=None, operands=(), second=None, second_operands=()):
    n = lax.axis_size("head")

    def exchange(x):
        return [head_peer(x, k) for k in range(1, n)]

    if work is None:
        return jnp.concatenate([own] + exchange(own), axis=0)
    if second is None:
        got, done = beside(exchange, own, work, operands)
        return jnp.concatenate([own] + got, axis=0), done
    own, operands = barrier((own, operands))
    got = exchange(own)
    done = work(*operands)
    got[0], second_operands = barrier((got[0], second_operands))
    got, done, also = barrier((got, done, second(*second_operands)))
    return jnp.concatenate([own] + got, axis=0), done, also


def gather_features(own, work=lambda: (), operands=()):
    n = lax.axis_size("head")
    part = own.shape[1] // n

    def exchange(x):
        return [head_peer(x, k) for k in range(1, n)]

    received, done = beside(exchange, own, work, operands)
    out = [own]
    for k, got in enumerate(received, 1):
        out.append(
            jnp.concatenate(
                [got[:, (j ^ k) * part : ((j ^ k) + 1) * part] for j in range(n)], axis=1
            )
        )
    return jnp.concatenate(out, axis=0), done


def peer_order(x):
    n = lax.axis_size("head")
    me = lax.axis_index("head")
    part = x.shape[0] // n
    return jnp.concatenate(
        [lax.dynamic_slice_in_dim(x, (me ^ k) * part, part, 0) for k in range(n)], axis=0
    )


def seq_blocks(x):
    n = lax.axis_size("seq")
    return [x] + [seq_shift(x, k) for k in range(1, n)]


def seq_slots(x):
    return jnp.stack(seq_blocks(x), axis=0)


def to_heads(x, work, operands=(), held=()):
    n = lax.axis_size("seq")
    me = lax.axis_index("seq")

    def exchange(x):
        def block(k):
            return lax.dynamic_index_in_dim(x, (me + k) % n, 0, keepdims=False)

        return [block(0)] + [seq_shift(block(k), k) for k in range(1, n)]

    x, operands = barrier((x, operands))
    got = exchange(x)
    got[1], held = barrier((got[1], held))
    got, done = barrier((got, work(*operands)))
    return jnp.stack(got, axis=0), done, held


def to_tokens(x, work, operands=(), second=lambda: (), second_operands=()):
    n = lax.axis_size("seq")
    me = lax.axis_index("seq")

    def exchange(x):
        return [x[0]] + [seq_shift(x[k], -k) for k in range(1, n)]

    x, operands = barrier((x, operands))
    got = exchange(x)
    done = work(*operands)
    got[1], second_operands = barrier((got[1], second_operands))
    got, done, also = barrier((got, done, second(*second_operands)))
    parts = jnp.stack(got, axis=0)
    out = [lax.dynamic_index_in_dim(parts, (h - me) % n, 0, keepdims=False) for h in range(n)]
    return jnp.stack(out, axis=0), done, also


def visible(block, xor, lo_token, queries, size):
    rows = lax.broadcasted_iota(jnp.int32, (size, 1), 0)
    keys = block * size + (rows ^ xor)
    return (keys <= queries) & (keys >= lo_token)


def attend_kernel(lo, qslot, kslot, base, q_ref, k_ref, v_ref, pos_ref, o_ref, ob_ref, lse_ref, kt_ref):
    i = pl.program_id(1)
    size = q_ref.shape[-1]
    blocks = k_ref.shape[1]

    @pl.when(i == 0)
    def _():
        for j in range(blocks):
            kt_ref[j] = jnp.transpose(k_ref[0, j, 0])

    xor = base[1]
    here = base[0] + i
    query = (q_ref[0, 0, 0].astype(F32) * SCALE).astype(BF16)
    lanes = lax.broadcasted_iota(jnp.int32, (1, size), 1)
    index = here * size + (lanes ^ xor)
    first = index - pos_ref[0]

    def step(j, carry):
        peak, total, acc = carry
        slot = kslot[j]
        s = dot(kt_ref[slot], query, ((1,), (0,)))
        s = jnp.where(visible(j, xor, first, index, size), s, MASKED)
        fresh = jnp.maximum(peak, jnp.max(s, axis=0, keepdims=True))
        p = jnp.exp(s - fresh)
        shrink = jnp.exp(peak - fresh)
        total = total * shrink + jnp.sum(p, axis=0, keepdims=True)
        acc = acc * shrink + dot(v_ref[0, slot, 0], p.astype(BF16), ((1,), (0,)))
        return fresh, total, acc

    peak, total, acc = lax.fori_loop(
        lo[i],
        here + 1,
        step,
        (
            jnp.full((1, size), MASKED, F32),
            jnp.zeros((1, size), F32),
            jnp.zeros((HEAD_DIM, size), F32),
        ),
    )
    out = acc / total
    o_ref[0, 0] = out
    ob_ref[0, 0] = out.astype(BF16)
    lse_ref[0, 0] = peak + jnp.log(total)


def grad_kernel(
    lo, qslot, kslot, base,
    q_ref, k_ref, v_ref, pos_ref, o_ref, dob_ref, lse_ref,
    dq_ref, dk_ref, dv_ref, kt_ref, vt_ref,
):
    i = pl.program_id(1)
    size = q_ref.shape[-1]
    blocks = k_ref.shape[1]

    @pl.when(i == 0)
    def _():
        for j in range(blocks):
            kt_ref[j] = jnp.transpose(k_ref[0, j, 0])
            vt_ref[j] = jnp.transpose(v_ref[0, j, 0])
        dk_ref[...] = jnp.zeros_like(dk_ref)
        dv_ref[...] = jnp.zeros_like(dv_ref)

    xor = base[1]
    here = base[0] + i
    query = (q_ref[0, 0, 0].astype(F32) * SCALE).astype(BF16)
    dob = dob_ref[0, 0]
    lse = lse_ref[0, 0]
    delta = jnp.sum(dob.astype(F32) * o_ref[0, 0], axis=0, keepdims=True)
    lanes = lax.broadcasted_iota(jnp.int32, (1, size), 1)
    index = here * size + (lanes ^ xor)
    first = index - pos_ref[0]

    def step(j, dq):
        slot = kslot[j]
        s = dot(kt_ref[slot], query, ((1,), (0,)))
        p = jnp.where(visible(j, xor, first, index, size), jnp.exp(s - lse), 0.0)
        dp = dot(vt_ref[slot], dob, ((1,), (0,)))
        ds = (p * (dp - delta)).astype(BF16)
        dv_ref[0, slot] += dot(dob, p.astype(BF16), ((1,), (1,)))
        dk_ref[0, slot] += dot(query, ds, ((1,), (1,)))
        return dq + dot(k_ref[0, slot, 0], ds, ((1,), (0,)))

    dq = lax.fori_loop(lo[i], here + 1, step, jnp.zeros((HEAD_DIM, size), F32))
    dq_ref[0, 0] = dq * SCALE


def attention_specs(heads, queries, keys, size):
    def q_at(h, i, lo, qslot, kslot, base):
        return (h, qslot[i], 0, 0, 0)

    def k_at(h, i, *_):
        return (h, 0, 1, 0, 0)

    def v_at(h, i, *_):
        return (h, 0, 2, 0, 0)

    def row_at(h, i, lo, qslot, kslot, base):
        return (qslot[i], 0, 0)

    def own_at(h, i, lo, qslot, kslot, base):
        return (h, qslot[i], 0, 0)

    q_spec = pl.BlockSpec((1, 1, 1, HEAD_DIM, size), q_at)
    k_spec = pl.BlockSpec((1, keys, 1, HEAD_DIM, size), k_at)
    v_spec = pl.BlockSpec((1, keys, 1, HEAD_DIM, size), v_at)
    pos_spec = pl.BlockSpec((1, 1, size), row_at)
    wide = pl.BlockSpec((1, 1, HEAD_DIM, size), own_at)
    thin = pl.BlockSpec((1, 1, 1, size), own_at)
    full = pl.BlockSpec((1, keys, HEAD_DIM, size), lambda h, i, *_: (h, 0, 0, 0))
    return q_spec, k_spec, v_spec, pos_spec, wide, thin, full


def attend(scalars, q, kv, pos):
    heads, queries, _, _, size = q.shape
    keys = kv.shape[1]
    q_spec, k_spec, v_spec, pos_spec, wide, thin, full = attention_specs(heads, queries, keys, size)
    pairs = heads * queries * keys * size * size
    return pl.pallas_call(
        attend_kernel,
        grid_spec=pltpu.PrefetchScalarGridSpec(
            num_scalar_prefetch=4,
            grid=(heads, queries),
            in_specs=[q_spec, k_spec, v_spec, pos_spec],
            out_specs=[wide, wide, thin],
            scratch_shapes=[pltpu.VMEM((keys, size, HEAD_DIM), BF16)],
        ),
        out_shape=[
            jax.ShapeDtypeStruct((heads, queries, HEAD_DIM, size), F32),
            jax.ShapeDtypeStruct((heads, queries, HEAD_DIM, size), BF16),
            jax.ShapeDtypeStruct((heads, queries, 1, size), F32),
        ],
        compiler_params=pltpu.CompilerParams(vmem_limit_bytes=40 << 20),
        cost_estimate=pl.CostEstimate(
            flops=4 * pairs * HEAD_DIM, bytes_accessed=4 * q.size, transcendentals=pairs
        ),
        name="attend",
    )(*scalars, q, kv, kv, pos)


def attend_grad(scalars, q, kv, pos, o, dob, lse):
    heads, queries, _, _, size = q.shape
    keys = kv.shape[1]
    q_spec, k_spec, v_spec, pos_spec, wide, thin, full = attention_specs(heads, queries, keys, size)
    pairs = heads * queries * keys * size * size
    return pl.pallas_call(
        grad_kernel,
        grid_spec=pltpu.PrefetchScalarGridSpec(
            num_scalar_prefetch=4,
            grid=(heads, queries),
            in_specs=[q_spec, k_spec, v_spec, pos_spec, wide, wide, thin],
            out_specs=[wide, full, full],
            scratch_shapes=[pltpu.VMEM((keys, size, HEAD_DIM), BF16)] * 2,
        ),
        out_shape=[
            jax.ShapeDtypeStruct((heads, queries, HEAD_DIM, size), F32),
            jax.ShapeDtypeStruct((heads, keys, HEAD_DIM, size), F32),
            jax.ShapeDtypeStruct((heads, keys, HEAD_DIM, size), F32),
        ],
        compiler_params=pltpu.CompilerParams(vmem_limit_bytes=48 << 20),
        cost_estimate=pl.CostEstimate(
            flops=10 * pairs * HEAD_DIM, bytes_accessed=8 * q.size, transcendentals=pairs
        ),
        name="attend_grad",
    )(*scalars, q, kv, kv, pos, o, dob, lse)


def turn(w, cosine, sine):
    first, second = w[..., :HALF, :], w[..., HALF:, :]
    return jnp.concatenate(
        [first * cosine - second * sine, second * cosine + first * sine], axis=-2
    )


def turn_back(w, cosine, sine):
    first, second = w[..., :HALF, :], w[..., HALF:, :]
    return jnp.concatenate(
        [first * cosine + second * sine, second * cosine - first * sine], axis=-2
    )


def half_rows(x, which):
    half = x.shape[0] // 2
    return lax.dynamic_slice_in_dim(x, which * half, half, 0)


def split_layers(shard):
    core = lax.axis_index("section")
    mine = half_rows(shard, core)
    got = core_swap(half_rows(shard, 1 - core))
    return jnp.where(core == 0, mine, got), jnp.where(core == 0, got, mine)


def gather_rows(half):
    return lax.all_gather(by_rows(half), ("seq", "section"), axis=0, tiled=True)


def join_halves(mine, in_slots):
    core = lax.axis_index("section")
    seq = lax.axis_index("seq")
    n = mine.shape[0]
    both = jnp.stack([mine, core_swap(mine)], axis=1).reshape(2 * n, *mine.shape[1:])
    return jnp.concatenate(
        [
            lax.dynamic_index_in_dim(
                both, ((seq - j) % n if in_slots else j) * 2 + (core ^ h), 0, keepdims=False
            )
            for j in range(n)
            for h in range(2)
        ],
        axis=0,
    )


def gather_peers(mine):
    n = lax.axis_size("head")
    return jnp.concatenate([mine] + [head_peer(mine, k) for k in range(1, n)], axis=-1)


def by_rows(x):
    return with_layout_constraint(x, Layout(tuple(range(x.ndim))))


def columns(x, *widths):
    out = []
    at = 0
    for w in widths:
        out.append(x[:, at : at + w])
        at += w
    return out


def scatter_rows(grad):
    return lax.psum_scatter(by_rows(grad), ("seq", "section"), scatter_dimension=0, tiled=True)


def add_cores(grad):
    core = lax.axis_index("section")
    n = lax.axis_size("seq")
    grad = grad.reshape(n, 2, grad.shape[0] // (2 * n), grad.shape[1])
    mine = lax.dynamic_index_in_dim(grad, core, 1, keepdims=False)
    other = core_swap(lax.dynamic_index_in_dim(grad, 1 - core, 1, keepdims=False))
    return (mine.astype(F32) + other.astype(F32)).astype(BF16)


def scatter_devices(total):
    seq = lax.axis_index("seq")
    n = lax.axis_size("seq")

    def block(k):
        return lax.dynamic_index_in_dim(total, (seq + k) % n, 0, keepdims=False)

    return [block(0)] + [seq_shift(block(k), k) for k in range(1, n)]


def add_up(parts):
    return sum((p.astype(F32) for p in parts[1:]), parts[0].astype(F32)).astype(BF16)


def on_device(
    inputs, positions, cotangent, qkv_weight, out_weight, gate_up_weight, down_weight,
    attn_gain, ffn_gain,
):
    core = lax.axis_index("section")
    seq = lax.axis_index("seq")
    devices = lax.axis_size("seq")
    peers = lax.axis_size("head")
    _, rows, width = inputs.shape
    part = rows // peers
    heads = qkv_weight.shape[3] // HEAD_DIM
    local = heads * HEAD_DIM
    hidden = down_weight.shape[2]
    by_head = devices == heads

    own = width // devices
    qkv_shard = (
        qkv_weight[0].reshape(own, 3, heads, HEAD_DIM).transpose(0, 2, 1, 3).reshape(own, 3 * local)
    )
    attn_shard = jnp.concatenate([qkv_shard, out_weight[0]], axis=1)
    attn_half, attn_later = split_layers(attn_shard)
    pos = lax.dynamic_index_in_dim(positions, core, 0, keepdims=False)
    gain = jnp.stack([attn_gain[0], ffn_gain[0]]).astype(F32)
    gain_other = core_swap(gain)
    small = jnp.where(core == 0, jnp.stack([gain, gain_other]), jnp.stack([gain_other, gain]))
    small = jnp.concatenate([peer_order(pos).astype(F32), small.reshape(4 * own)])
    small = seq_slots(small)
    attn_half, inputs, cotangent, gate_up_weight, down_weight = barrier(
        (attn_half, inputs, cotangent, gate_up_weight, down_weight)
    )
    first = seq_blocks(attn_half)
    ffn_shard = jnp.concatenate(
        [gate_up_weight[0].reshape(own, 2 * hidden), down_weight[0]], axis=1
    )
    ffn_half, ffn_later = split_layers(by_rows(ffn_shard))
    first = jnp.stack(first, axis=0)
    w_qkv_first = join_halves(first[:, :, : 3 * local], True)
    out_first = first[:, :, 3 * local :]
    gain = small[:, rows:].reshape(devices, 2, 2, own)
    gain = jnp.stack(
        [
            lax.dynamic_index_in_dim(gain, (seq - j) % devices, 0, keepdims=False)
            for j in range(devices)
        ],
        axis=2,
    ).reshape(2, 2, width)

    x0 = peer_order(lax.dynamic_index_in_dim(inputs, core, 0, keepdims=False))
    gy1 = peer_order(lax.dynamic_index_in_dim(cotangent, core, 0, keepdims=False))
    pos = small[:, :rows].astype(jnp.int32)
    xor = lax.axis_index("head") * part
    slots = (seq - jnp.arange(devices, dtype=jnp.int32)) % devices
    token = slots[:, None] * rows + (jnp.arange(rows, dtype=jnp.int32) ^ xor)[None, :]
    lowest = jnp.min(token - pos, axis=1) // rows
    rates = 10000.0 ** (-jnp.arange(HALF, dtype=F32) / HALF)
    theta = pos.astype(F32)[:, None, :] * rates[None, :, None]
    cosine, sine = jnp.cos(theta), jnp.sin(theta)
    own_cos, own_sin = cosine[0], sine[0]
    if by_head:
        scalars = (
            lowest[slots],
            slots,
            slots,
            jnp.stack([jnp.zeros((), jnp.int32), xor]),
        )
        pos_rows = pos[:, None, :]
        back_cos, back_sin = cosine, sine
    else:
        scalars = (
            lowest[:1],
            jnp.zeros((1,), jnp.int32),
            jnp.arange(devices, dtype=jnp.int32),
            jnp.stack([seq, xor]),
        )
        pos_rows = pos[:1, None, :]
        back_cos, back_sin = own_cos, own_sin

    def norm(v, g):
        inverse = lax.rsqrt(jnp.mean(v * v, axis=-1, keepdims=True) + EPS)
        return inverse, (v * inverse * g).astype(BF16)

    def project(layer, x, w_qkv, first_value):
        x_full = x.astype(F32)
        _, n1 = norm(x_full, gain[layer, 0])
        p = dot(w_qkv, n1, ((0,), (1,))).reshape(heads, 3, HEAD_DIM, rows)
        q = turn(p[:, 0], own_cos, own_sin).astype(BF16)
        k = turn(p[:, 1], own_cos, own_sin).astype(BF16)
        v = p[:, 2]
        if first_value is not None:
            v = 0.5 * v + 0.5 * first_value.astype(F32)
        v = v.astype(BF16)
        return n1, jnp.stack([q, k, v], axis=1), v

    def mix(packed, out_mine, in_slots, held):
        if by_head:
            query, out_all, _ = to_heads(packed, gather_peers, (out_mine,))
            query = query[None]
            key_value = query
        else:
            out_all = gather_peers(out_mine)
            query = packed[:, None]
            key_value = jnp.transpose(lax.all_gather(packed, "seq"), (1, 0, 2, 3, 4))
        key_value, held = barrier((key_value, held))
        query = key_value if by_head else query
        o, ob, lse = attend(scalars, query, key_value, pos_rows)

        def join(out_all):
            return join_halves(out_all, in_slots)

        if by_head:
            ob, w_out, _ = to_tokens(ob[0], join, (out_all,))
        else:
            ob, w_out = ob[:, 0], join(out_all)
        return ob.reshape(local, rows), w_out, (query, key_value, o, lse), held

    def feed(layer, x, ob_all, w_out, w_gate_up, w_down):
        hid = x.astype(F32) + dot(ob_all, w_out, ((0,), (1,)))
        r2, n2 = norm(hid, gain[layer, 1])
        gate_up = dot(n2, w_gate_up, ((1,), (0,)))
        gate, up = gate_up[:, :hidden], gate_up[:, hidden:]
        act = (jax.nn.silu(gate) * up).astype(BF16)
        y_part = dot(act, w_down, ((1,), (1,))).astype(BF16)
        return y_part, (hid[:part], r2[:part], n2, gate, up, act)

    def to_first(value):
        return lax.ppermute(value, "section", [(1, 0)])

    def to_second(value):
        return lax.ppermute(value, "section", [(0, 1)])

    def to_second_all(*values):
        return [to_second(v) for v in values]

    def settle(first_layer, first_other, second_layer, second_other):
        return (
            jnp.where(core == 0, first_layer, second_other),
            jnp.where(core == 0, first_other, second_layer),
        )

    def place(first_layer, second_layer):
        return settle(first_layer, to_first(first_layer), second_layer, to_second(second_layer))

    def add_peers(gains):
        return sum((head_peer(gains, k) for k in range(1, peers)), gains)

    def backward(layer, gyb, gfirst, kept, late, before):
        x_own, n1, (query, key_value, o, lse), ob, w_out, fed, w_qkv, w_gate_up, w_down = kept
        hid, r2, n2, gate, up, act = fed
        sigmoid = jax.nn.sigmoid(gate)
        da = dot(gyb, w_down, ((1,), (0,)))
        dgate = da * up * sigmoid * (1.0 + gate * (1.0 - sigmoid))
        dup = da * (gate * sigmoid)
        dgu = jnp.concatenate([dgate, dup], axis=1).astype(BF16)

        def grad_rows(a, b):
            return dot(a, b, ((0,), (0,))).astype(BF16)

        def gain_rows(dn, n, g):
            return jnp.sum(dn.astype(F32) * n.astype(F32), axis=0) / g

        def beside_ffn(dn, n2, dgu):
            g_gate_up, g_gain = grad_rows(n2, dgu), gain_rows(dn, n2, gain[layer, 1])
            if layer:
                return g_gate_up, g_gain
            g_gate_up = by_rows(jnp.concatenate([g_gate_up, before[1]], axis=1))
            return g_gate_up, g_gain, to_second(before[3])

        dn2 = dot(dgu, w_gate_up, ((1,), (1,))).astype(BF16)
        dn2, (g_gate_up, g_ffn_gain, *y_other) = reduce_tokens(dn2, beside_ffn, (dn2, n2, dgu))
        c2 = hid * r2
        e2 = dn2 * gain[layer, 1]
        gh = gyb[:part].astype(F32) + r2 * (e2 - c2 * jnp.mean(e2 * c2, axis=-1, keepdims=True))
        ghb, g_gate_up = barrier((gh.astype(BF16), g_gate_up))
        gate_up_rows = scatter_rows(g_gate_up)

        def beside_ghb(gyb, act):
            return (grad_rows(gyb, act), *(() if layer else (to_second(gyb),)))

        ghb, (g_down, *gx_other) = gather_tokens(ghb, beside_ghb, (gyb, act))
        dob = dot(w_out[:, :local], ghb, ((0,), (1,))).astype(BF16)
        dob = dob.reshape(heads, HEAD_DIM, rows)

        def grad_rest(ghb, ob, g_down):
            g_out = dot(ghb, ob, ((0,), (1,))).astype(BF16)
            return jnp.concatenate([g_out, g_down], axis=1)

        if by_head:
            dob, g_rest, late = to_heads(dob, grad_rest, (ghb, ob, g_down), late)
            dob = dob[None]
        else:
            g_rest = grad_rest(ghb, ob, g_down)
            dob = dob[:, None]
        dob, g_rest = barrier((dob, g_rest))
        rest_rows = scatter_rows(g_rest)
        if layer:
            y_part, y_hid = late
            y_own = (y_hid + reduce_tokens(y_part)).astype(BF16)
        dq, dk, dv = attend_grad(scalars, query, key_value, pos_rows, o, dob, lse)
        if layer:
            dq, y_own = barrier((dq, y_own))
        if by_head:
            dq, dk, dv = dq[0], dk[0], dv[0]
        else:
            dq = dq[:, 0]
            dkv = jnp.stack([dk, dv], axis=1).transpose(2, 0, 1, 3, 4).astype(BF16)
            dkv = lax.psum_scatter(dkv, "seq", scatter_dimension=0, tiled=False).astype(F32)
            dk, dv = dkv[:, 0], dkv[:, 1]
        dq = turn_back(dq, back_cos, back_sin).astype(BF16)
        dk = turn_back(dk, back_cos, back_sin).astype(BF16)
        if gfirst is None:
            dv = (0.5 * dv).astype(BF16)
        else:
            dv = (dv + gfirst.astype(F32)).astype(BF16)
        packed = jnp.stack([dq, dk, dv], axis=1)
        if by_head and layer:
            packed, _, y = to_tokens(packed, lambda: (), (), gather_tokens, (y_own,))
        elif by_head:
            packed, _, rows_other = to_tokens(packed, lambda: (), (), to_second_all, before[0])
        elif layer:
            y = gather_tokens(y_own)
        else:
            rows_other = to_second_all(*before[0])
        dqkv = packed.reshape(3 * local, rows)

        dn1 = dot(dqkv, w_qkv, ((0,), (1,))).astype(BF16)
        g_attn_gain = gain_rows(dn1, n1, gain[layer, 0])
        gains = jnp.stack([g_attn_gain, g_ffn_gain])

        def grad_qkv(n1, dqkv):
            g_qkv = dot(n1, dqkv, ((0,), (1,))).astype(BF16)
            return g_qkv if layer else scatter_devices(add_cores(g_qkv))

        if layer:
            dn1, g_qkv = reduce_tokens(dn1, grad_qkv, (n1, dqkv))
        else:
            gains = jnp.concatenate([gains, before[2]], axis=0)
            high = gains.astype(BF16)
            low = (gains - high.astype(F32)).astype(BF16)
            tail = jnp.concatenate([high, low, jnp.zeros((8, width), BF16)], axis=0)
            dn1 = jnp.concatenate([dn1.reshape(peers, part, width)] + [
                jnp.broadcast_to(tail[None], (peers, 16, width))
            ], axis=1).reshape(peers * (part + 16), width)
            dn1, n1, dqkv = barrier((dn1, n1, dqkv))
            qkv_parts = grad_qkv(n1, dqkv)
            dn1 = reduce_tokens(dn1)
            gains = dn1[part : part + 4] + dn1[part + 4 : part + 8]
            dn1 = dn1[:part]
        r1 = lax.rsqrt(jnp.mean(x_own * x_own, axis=-1, keepdims=True) + EPS)
        c1 = x_own * r1
        e1 = dn1 * gain[layer, 0]
        gx = gh + r1 * (e1 - c1 * jnp.mean(e1 * c1, axis=-1, keepdims=True))
        gx = gx.astype(BF16)
        if layer:
            return gather_tokens(gx), dv, (gate_up_rows, rest_rows), g_qkv, gains, y

        def beside_last(gate_up_rows, gains):
            gains = gains.reshape(2, 2, width)
            mine = lax.dynamic_index_in_dim(gains, core, 0, keepdims=False)
            other = lax.dynamic_index_in_dim(gains, 1 - core, 0, keepdims=False)
            gate_up, qkv = columns(gate_up_rows, 2 * hidden, 3 * local)
            gate_up = settle(gate_up, to_first(gate_up), before[0][0], rows_other[0])
            return rows_of(gate_up), qkv, to_second(qkv), mine + core_swap(other)

        def then(qkv_parts, gains):
            qkv = add_up(qkv_parts)
            return qkv, to_first(qkv), add_devices(gains)

        n = peers
        gx, gate_up_rows, gains = barrier((gx, gate_up_rows, gains))
        got = [head_peer(gx, k) for k in range(1, n)]
        gate_up, qkv1, qkv1_other, gains = beside_last(gate_up_rows, gains)
        got[0], qkv_parts, gains = barrier((got[0], qkv_parts, gains))
        qkv0, qkv0_other, gains = then(qkv_parts, gains)
        got, gate_up, qkv, gains, rest_rows = barrier(
            (got, gate_up, (qkv0, qkv0_other, qkv1, qkv1_other), gains, rest_rows)
        )
        gx = jnp.concatenate([gx] + got, axis=0)
        return gx, gate_up, qkv, gains, rest_rows, y_other[0], gx_other[0], rows_other[1]

    def rows_of(pair):
        return jnp.concatenate(pair, axis=0).astype(F32)

    def add_devices(gains):
        gains = gains.reshape(2, devices, own)
        mine = lax.dynamic_index_in_dim(gains, seq, 1, keepdims=False)
        for k in range(1, devices):
            block = lax.dynamic_index_in_dim(gains, (seq + k) % devices, 1, keepdims=False)
            mine = mine + seq_shift(block, k)
        return mine

    n1_0, packed, v0 = project(0, x0, w_qkv_first, None)
    ob0, w_out0, attn0, ffn_half = mix(packed, out_first, True, ffn_half)
    gate_up0, down0 = columns(gather_rows(ffn_half), 2 * hidden, hidden)
    ob0, attn_later = barrier((ob0, attn_later))
    attn_later = gather_rows(attn_later)
    y_part, fed0 = feed(0, x0, gather_features(ob0)[0], w_out0, gate_up0, down0)
    y0 = gather_tokens((fed0[0] + reduce_tokens(y_part)).astype(BF16))
    qkv1, out1 = columns(attn_later, 3 * local, local)
    out1 = lax.dynamic_index_in_dim(
        out1.reshape(devices, 2, own // 2, local), core, 1, keepdims=False
    )
    n1_1, packed, _ = project(1, y0, qkv1, v0)
    ob1, w_out1, attn1, ffn_later = mix(packed, out1, False, ffn_later)
    gate_up1, down1 = columns(gather_rows(ffn_later), 2 * hidden, hidden)
    ob_all, y0_first = gather_features(ob1, to_first, (y0,))
    y_part, fed1 = feed(1, y0, ob_all, w_out1, gate_up1, down1)
    kept0 = (x0[:part].astype(F32), n1_0, attn0, ob0, w_out0, fed0, w_qkv_first, gate_up0, down0)
    kept1 = (y0[:part].astype(F32), n1_1, attn1, ob1, w_out1, fed1, qkv1, gate_up1, down1)
    gx1, gfirst, rows1, g_qkv1, gains1, y1 = backward(
        1, gy1, None, kept1, (y_part, fed1[0]), ()
    )
    gx0, gate_up_grad, qkv, gains, rest_rows, y1_second, gx1_second, rest_second = backward(
        0, gx1, gfirst, kept0, (), (rows1, g_qkv1, gains1, y1)
    )

    def tokens_of(pair, dtype):
        return jnp.stack([peer_order(m).astype(dtype) for m in pair])[None]

    activations = tokens_of(settle(y0, y0_first, y1, y1_second), BF16)
    gx0_first, rest_first = to_first(gx0), to_first(rest_rows)
    input_grads = tokens_of(settle(gx0, gx0_first, gx1, gx1_second), F32)
    gate_up_grad = gate_up_grad.reshape(1, own, 2, hidden)
    qkv_grad = (
        rows_of(settle(*qkv))
        .reshape(1, own, heads, 3, HEAD_DIM)
        .transpose(0, 1, 3, 2, 4)
        .reshape(1, own, 3, local)
    )
    out_grad, down_grad = [
        g[None]
        for g in columns(
            rows_of(settle(rest_rows, rest_first, rows1[1], rest_second)), local, hidden
        )
    ]
    return (
        activations,
        input_grads,
        qkv_grad,
        out_grad,
        gate_up_grad,
        down_grad,
        gains[0][None],
        gains[1][None],
    )


def solution(mesh):
    placed = (
        P(None, "seq", None),
        P(None, "seq"),
        P(None, "seq", None),
        P("section", "seq", None, "head"),
        P("section", "seq", "head"),
        P("section", "seq", None, "head"),
        P("section", "seq", "head"),
        P("section", "seq"),
        P("section", "seq"),
    )
    return jax.shard_map(
        on_device,
        mesh=mesh,
        in_specs=placed,
        out_specs=(
            P("section", None, "seq", None),
            P("section", None, "seq", None),
            P("section", "seq", None, "head"),
            P("section", "seq", "head"),
            P("section", "seq", None, "head"),
            P("section", "seq", "head"),
            P("section", "seq"),
            P("section", "seq"),
        ),
        check_vma=False,
    )
```

```python
import jax
import jax.numpy as jnp
from jax import lax
from jax.experimental import pallas as pl
from jax.experimental.layout import Layout, with_layout_constraint
from jax.experimental.pallas import tpu as pltpu
from jax.sharding import PartitionSpec as P

HEAD_DIM = 64
HALF = HEAD_DIM // 2
EPS = 1e-06
MASKED = -1e30
SCALE = HEAD_DIM ** (-0.5)
BF16 = jnp.bfloat16
F32 = jnp.float32


def dot(a, b, dims):
    return lax.dot_general(a, b, (dims, ((), ())), preferred_element_type=F32)


def head_peer(x, k):
    n = lax.axis_size("head")
    return lax.ppermute(x, "head", [(i, i ^ k) for i in range(n)])


def seq_shift(x, k):
    n = lax.axis_size("seq")
    return lax.ppermute(x, "seq", [(i, (i + k) % n) for i in range(n)])


def core_swap(x):
    return lax.ppermute(x, "section", [(0, 1), (1, 0)])


barrier = lax.optimization_barrier


def beside(exchange, value, work, operands):
    value, operands = barrier((value, operands))
    got = exchange(value)
    done = work(*operands)
    return barrier((got, done))


def reduce_tokens(partial_sum, work=None, operands=()):
    n = lax.axis_size("head")
    part = partial_sum.shape[0] // n

    def exchange(low):
        return [head_peer(low[k * part : (k + 1) * part], k) for k in range(1, n)]

    low = partial_sum.astype(BF16)
    if work is None:
        got = exchange(low)
    else:
        got, done = beside(exchange, low, work, operands)
    total = low[:part].astype(F32)
    for g in got:
        total = total + g.astype(F32)
    return total if work is None else (total, done)


def gather_tokens(own, work=lambda: (), operands=()):
    n = lax.axis_size("head")

    def exchange(x):
        return [head_peer(x, k) for k in range(1, n)]

    got, done = beside(exchange, own, work, operands)
    return jnp.concatenate([own] + got, axis=0), done


def gather_features(own, work=lambda: (), operands=()):
    n = lax.axis_size("head")
    part = own.shape[1] // n

    def exchange(x):
        return [head_peer(x, k) for k in range(1, n)]

    received, done = beside(exchange, own, work, operands)
    out = [own]
    for k, got in enumerate(received, 1):
        out.append(
            jnp.concatenate(
                [got[:, (j ^ k) * part : ((j ^ k) + 1) * part] for j in range(n)], axis=1
            )
        )
    return jnp.concatenate(out, axis=0), done


def peer_order(x):
    n = lax.axis_size("head")
    me = lax.axis_index("head")
    part = x.shape[0] // n
    return jnp.concatenate(
        [lax.dynamic_slice_in_dim(x, (me ^ k) * part, part, 0) for k in range(n)], axis=0
    )


def seq_blocks(x):
    n = lax.axis_size("seq")
    return [x] + [seq_shift(x, k) for k in range(1, n)]


def seq_slots(x):
    return jnp.stack(seq_blocks(x), axis=0)


def to_heads(x, work, operands=()):
    n = lax.axis_size("seq")
    me = lax.axis_index("seq")

    def exchange(x):
        def block(k):
            return lax.dynamic_index_in_dim(x, (me + k) % n, 0, keepdims=False)

        return [block(0)] + [seq_shift(block(k), k) for k in range(1, n)]

    got, done = beside(exchange, x, work, operands)
    return jnp.stack(got, axis=0), done


def to_tokens(x, work, operands=()):
    n = lax.axis_size("seq")
    me = lax.axis_index("seq")

    def exchange(x):
        return [x[0]] + [seq_shift(x[k], -k) for k in range(1, n)]

    got, done = beside(exchange, x, work, operands)
    parts = jnp.stack(got, axis=0)
    out = [lax.dynamic_index_in_dim(parts, (h - me) % n, 0, keepdims=False) for h in range(n)]
    return jnp.stack(out, axis=0), done


def visible(block, xor, lo_token, queries, size):
    rows = lax.broadcasted_iota(jnp.int32, (size, 1), 0)
    keys = block * size + (rows ^ xor)
    return (keys <= queries) & (keys >= lo_token)


def attend_kernel(lo, qslot, kslot, base, q_ref, k_ref, v_ref, pos_ref, o_ref, ob_ref, lse_ref, kt_ref):
    i = pl.program_id(1)
    size = q_ref.shape[-1]
    blocks = k_ref.shape[1]

    @pl.when(i == 0)
    def _():
        for j in range(blocks):
            kt_ref[j] = jnp.transpose(k_ref[0, j, 0])

    xor = base[1]
    here = base[0] + i
    query = (q_ref[0, 0, 0].astype(F32) * SCALE).astype(BF16)
    lanes = lax.broadcasted_iota(jnp.int32, (1, size), 1)
    index = here * size + (lanes ^ xor)
    first = index - pos_ref[0]

    def step(j, carry):
        peak, total, acc = carry
        slot = kslot[j]
        s = dot(kt_ref[slot], query, ((1,), (0,)))
        s = jnp.where(visible(j, xor, first, index, size), s, MASKED)
        fresh = jnp.maximum(peak, jnp.max(s, axis=0, keepdims=True))
        p = jnp.exp(s - fresh)
        shrink = jnp.exp(peak - fresh)
        total = total * shrink + jnp.sum(p, axis=0, keepdims=True)
        acc = acc * shrink + dot(v_ref[0, slot, 0], p.astype(BF16), ((1,), (0,)))
        return fresh, total, acc

    peak, total, acc = lax.fori_loop(
        lo[i],
        here + 1,
        step,
        (
            jnp.full((1, size), MASKED, F32),
            jnp.zeros((1, size), F32),
            jnp.zeros((HEAD_DIM, size), F32),
        ),
    )
    out = acc / total
    o_ref[0, 0] = out
    ob_ref[0, 0] = out.astype(BF16)
    lse_ref[0, 0] = peak + jnp.log(total)


def grad_kernel(
    lo, qslot, kslot, base,
    q_ref, k_ref, v_ref, pos_ref, o_ref, dob_ref, lse_ref,
    dq_ref, dk_ref, dv_ref, kt_ref, vt_ref,
):
    i = pl.program_id(1)
    size = q_ref.shape[-1]
    blocks = k_ref.shape[1]

    @pl.when(i == 0)
    def _():
        for j in range(blocks):
            kt_ref[j] = jnp.transpose(k_ref[0, j, 0])
            vt_ref[j] = jnp.transpose(v_ref[0, j, 0])
        dk_ref[...] = jnp.zeros_like(dk_ref)
        dv_ref[...] = jnp.zeros_like(dv_ref)

    xor = base[1]
    here = base[0] + i
    query = (q_ref[0, 0, 0].astype(F32) * SCALE).astype(BF16)
    dob = dob_ref[0, 0]
    lse = lse_ref[0, 0]
    delta = jnp.sum(dob.astype(F32) * o_ref[0, 0], axis=0, keepdims=True)
    lanes = lax.broadcasted_iota(jnp.int32, (1, size), 1)
    index = here * size + (lanes ^ xor)
    first = index - pos_ref[0]

    def step(j, dq):
        slot = kslot[j]
        s = dot(kt_ref[slot], query, ((1,), (0,)))
        p = jnp.where(visible(j, xor, first, index, size), jnp.exp(s - lse), 0.0)
        dp = dot(vt_ref[slot], dob, ((1,), (0,)))
        ds = (p * (dp - delta)).astype(BF16)
        dv_ref[0, slot] += dot(dob, p.astype(BF16), ((1,), (1,)))
        dk_ref[0, slot] += dot(query, ds, ((1,), (1,)))
        return dq + dot(k_ref[0, slot, 0], ds, ((1,), (0,)))

    dq = lax.fori_loop(lo[i], here + 1, step, jnp.zeros((HEAD_DIM, size), F32))
    dq_ref[0, 0] = dq * SCALE


def attention_specs(heads, queries, keys, size):
    def q_at(h, i, lo, qslot, kslot, base):
        return (h, qslot[i], 0, 0, 0)

    def k_at(h, i, *_):
        return (h, 0, 1, 0, 0)

    def v_at(h, i, *_):
        return (h, 0, 2, 0, 0)

    def row_at(h, i, lo, qslot, kslot, base):
        return (qslot[i], 0, 0)

    def own_at(h, i, lo, qslot, kslot, base):
        return (h, qslot[i], 0, 0)

    q_spec = pl.BlockSpec((1, 1, 1, HEAD_DIM, size), q_at)
    k_spec = pl.BlockSpec((1, keys, 1, HEAD_DIM, size), k_at)
    v_spec = pl.BlockSpec((1, keys, 1, HEAD_DIM, size), v_at)
    pos_spec = pl.BlockSpec((1, 1, size), row_at)
    wide = pl.BlockSpec((1, 1, HEAD_DIM, size), own_at)
    thin = pl.BlockSpec((1, 1, 1, size), own_at)
    full = pl.BlockSpec((1, keys, HEAD_DIM, size), lambda h, i, *_: (h, 0, 0, 0))
    return q_spec, k_spec, v_spec, pos_spec, wide, thin, full


def attend(scalars, q, kv, pos):
    heads, queries, _, _, size = q.shape
    keys = kv.shape[1]
    q_spec, k_spec, v_spec, pos_spec, wide, thin, full = attention_specs(heads, queries, keys, size)
    pairs = heads * queries * keys * size * size
    return pl.pallas_call(
        attend_kernel,
        grid_spec=pltpu.PrefetchScalarGridSpec(
            num_scalar_prefetch=4,
            grid=(heads, queries),
            in_specs=[q_spec, k_spec, v_spec, pos_spec],
            out_specs=[wide, wide, thin],
            scratch_shapes=[pltpu.VMEM((keys, size, HEAD_DIM), BF16)],
        ),
        out_shape=[
            jax.ShapeDtypeStruct((heads, queries, HEAD_DIM, size), F32),
            jax.ShapeDtypeStruct((heads, queries, HEAD_DIM, size), BF16),
            jax.ShapeDtypeStruct((heads, queries, 1, size), F32),
        ],
        compiler_params=pltpu.CompilerParams(vmem_limit_bytes=40 << 20),
        cost_estimate=pl.CostEstimate(
            flops=4 * pairs * HEAD_DIM, bytes_accessed=4 * q.size, transcendentals=pairs
        ),
        name="attend",
    )(*scalars, q, kv, kv, pos)


def attend_grad(scalars, q, kv, pos, o, dob, lse):
    heads, queries, _, _, size = q.shape
    keys = kv.shape[1]
    q_spec, k_spec, v_spec, pos_spec, wide, thin, full = attention_specs(heads, queries, keys, size)
    pairs = heads * queries * keys * size * size
    return pl.pallas_call(
        grad_kernel,
        grid_spec=pltpu.PrefetchScalarGridSpec(
            num_scalar_prefetch=4,
            grid=(heads, queries),
            in_specs=[q_spec, k_spec, v_spec, pos_spec, wide, wide, thin],
            out_specs=[wide, full, full],
            scratch_shapes=[pltpu.VMEM((keys, size, HEAD_DIM), BF16)] * 2,
        ),
        out_shape=[
            jax.ShapeDtypeStruct((heads, queries, HEAD_DIM, size), F32),
            jax.ShapeDtypeStruct((heads, keys, HEAD_DIM, size), F32),
            jax.ShapeDtypeStruct((heads, keys, HEAD_DIM, size), F32),
        ],
        compiler_params=pltpu.CompilerParams(vmem_limit_bytes=48 << 20),
        cost_estimate=pl.CostEstimate(
            flops=10 * pairs * HEAD_DIM, bytes_accessed=8 * q.size, transcendentals=pairs
        ),
        name="attend_grad",
    )(*scalars, q, kv, kv, pos, o, dob, lse)


def turn(w, cosine, sine):
    first, second = w[..., :HALF, :], w[..., HALF:, :]
    return jnp.concatenate(
        [first * cosine - second * sine, second * cosine + first * sine], axis=-2
    )


def turn_back(w, cosine, sine):
    first, second = w[..., :HALF, :], w[..., HALF:, :]
    return jnp.concatenate(
        [first * cosine + second * sine, second * cosine - first * sine], axis=-2
    )


def half_rows(x, which):
    half = x.shape[0] // 2
    return lax.dynamic_slice_in_dim(x, which * half, half, 0)


def split_layers(shard):
    core = lax.axis_index("section")
    mine = half_rows(shard, core)
    got = core_swap(half_rows(shard, 1 - core))
    return jnp.where(core == 0, mine, got), jnp.where(core == 0, got, mine)


def gather_rows(half):
    return lax.all_gather(by_rows(half), ("seq", "section"), axis=0, tiled=True)


def join_halves(mine, in_slots):
    core = lax.axis_index("section")
    seq = lax.axis_index("seq")
    n = mine.shape[0]
    both = jnp.stack([mine, core_swap(mine)], axis=1).reshape(2 * n, *mine.shape[1:])
    return jnp.concatenate(
        [
            lax.dynamic_index_in_dim(
                both, ((seq - j) % n if in_slots else j) * 2 + (core ^ h), 0, keepdims=False
            )
            for j in range(n)
            for h in range(2)
        ],
        axis=0,
    )


def gather_peers(mine):
    n = lax.axis_size("head")
    return jnp.concatenate([mine] + [head_peer(mine, k) for k in range(1, n)], axis=-1)


def by_rows(x):
    return with_layout_constraint(x, Layout(tuple(range(x.ndim))))


def columns(x, *widths):
    out = []
    at = 0
    for w in widths:
        out.append(x[:, at : at + w])
        at += w
    return out


def scatter_rows(grad):
    return lax.psum_scatter(by_rows(grad), ("seq", "section"), scatter_dimension=0, tiled=True)


def on_device(
    inputs, positions, cotangent, qkv_weight, out_weight, gate_up_weight, down_weight,
    attn_gain, ffn_gain,
):
    core = lax.axis_index("section")
    seq = lax.axis_index("seq")
    devices = lax.axis_size("seq")
    peers = lax.axis_size("head")
    _, rows, width = inputs.shape
    part = rows // peers
    heads = qkv_weight.shape[3] // HEAD_DIM
    local = heads * HEAD_DIM
    hidden = down_weight.shape[2]
    by_head = devices == heads

    own = width // devices
    qkv_shard = (
        qkv_weight[0].reshape(own, 3, heads, HEAD_DIM).transpose(0, 2, 1, 3).reshape(own, 3 * local)
    )
    attn_shard = jnp.concatenate([qkv_shard, out_weight[0]], axis=1)
    attn_half, attn_later = split_layers(attn_shard)
    (
        attn_half, inputs, cotangent, positions, gate_up_weight, down_weight, attn_gain, ffn_gain,
    ) = barrier(
        (attn_half, inputs, cotangent, positions, gate_up_weight, down_weight, attn_gain, ffn_gain)
    )
    first = seq_blocks(attn_half)
    pos = lax.dynamic_index_in_dim(positions, core, 0, keepdims=False)
    gain = jnp.stack([attn_gain[0], ffn_gain[0]]).astype(F32)
    gain_other = core_swap(gain)
    small = jnp.where(core == 0, jnp.stack([gain, gain_other]), jnp.stack([gain_other, gain]))
    small = jnp.concatenate([peer_order(pos).astype(F32), small.reshape(4 * own)])
    small = seq_slots(small)
    ffn_shard = jnp.concatenate(
        [gate_up_weight[0].reshape(own, 2 * hidden), down_weight[0]], axis=1
    )
    ffn_half, ffn_later = split_layers(by_rows(ffn_shard))
    first = jnp.stack(first, axis=0)
    w_qkv_first = join_halves(first[:, :, : 3 * local], True)
    out_first = first[:, :, 3 * local :]
    gain = small[:, rows:].reshape(devices, 2, 2, own)
    gain = jnp.stack(
        [
            lax.dynamic_index_in_dim(gain, (seq - j) % devices, 0, keepdims=False)
            for j in range(devices)
        ],
        axis=2,
    ).reshape(2, 2, width)

    x0 = peer_order(lax.dynamic_index_in_dim(inputs, core, 0, keepdims=False))
    gy1 = peer_order(lax.dynamic_index_in_dim(cotangent, core, 0, keepdims=False))
    pos = small[:, :rows].astype(jnp.int32)
    xor = lax.axis_index("head") * part
    slots = (seq - jnp.arange(devices, dtype=jnp.int32)) % devices
    token = slots[:, None] * rows + (jnp.arange(rows, dtype=jnp.int32) ^ xor)[None, :]
    lowest = jnp.min(token - pos, axis=1) // rows
    rates = 10000.0 ** (-jnp.arange(HALF, dtype=F32) / HALF)
    theta = pos.astype(F32)[:, None, :] * rates[None, :, None]
    cosine, sine = jnp.cos(theta), jnp.sin(theta)
    own_cos, own_sin = cosine[0], sine[0]
    if by_head:
        scalars = (
            lowest[slots],
            slots,
            slots,
            jnp.stack([jnp.zeros((), jnp.int32), xor]),
        )
        pos_rows = pos[:, None, :]
        back_cos, back_sin = cosine, sine
    else:
        scalars = (
            lowest[:1],
            jnp.zeros((1,), jnp.int32),
            jnp.arange(devices, dtype=jnp.int32),
            jnp.stack([seq, xor]),
        )
        pos_rows = pos[:1, None, :]
        back_cos, back_sin = own_cos, own_sin

    def norm(v, g):
        inverse = lax.rsqrt(jnp.mean(v * v, axis=-1, keepdims=True) + EPS)
        return inverse, (v * inverse * g).astype(BF16)

    def project(layer, x, w_qkv, first_value):
        x_full = x.astype(F32)
        _, n1 = norm(x_full, gain[layer, 0])
        p = dot(w_qkv, n1, ((0,), (1,))).reshape(heads, 3, HEAD_DIM, rows)
        q = turn(p[:, 0], own_cos, own_sin).astype(BF16)
        k = turn(p[:, 1], own_cos, own_sin).astype(BF16)
        v = p[:, 2]
        if first_value is not None:
            v = 0.5 * v + 0.5 * first_value.astype(F32)
        v = v.astype(BF16)
        return n1, jnp.stack([q, k, v], axis=1), v

    def mix(packed, out_mine, in_slots, held):
        if by_head:
            query, out_all = to_heads(packed, gather_peers, (out_mine,))
            query = query[None]
            key_value = query
        else:
            out_all = gather_peers(out_mine)
            query = packed[:, None]
            key_value = jnp.transpose(lax.all_gather(packed, "seq"), (1, 0, 2, 3, 4))
        key_value, held = barrier((key_value, held))
        query = key_value if by_head else query
        o, ob, lse = attend(scalars, query, key_value, pos_rows)

        def join(out_all):
            return join_halves(out_all, in_slots)

        if by_head:
            ob, w_out = to_tokens(ob[0], join, (out_all,))
        else:
            ob, w_out = ob[:, 0], join(out_all)
        return ob.reshape(local, rows), w_out, (query, key_value, o, lse), held

    def feed(layer, x, ob_all, w_out, w_gate_up, w_down):
        hid = x.astype(F32) + dot(ob_all, w_out, ((0,), (1,)))
        r2, n2 = norm(hid, gain[layer, 1])
        gate_up = dot(n2, w_gate_up, ((1,), (0,)))
        gate, up = gate_up[:, :hidden], gate_up[:, hidden:]
        act = (jax.nn.silu(gate) * up).astype(BF16)
        y_part = dot(act, w_down, ((1,), (1,))).astype(BF16)
        return y_part, (hid[:part], r2[:part], n2, gate, up, act)

    def to_first(value):
        return lax.ppermute(value, "section", [(1, 0)])

    def to_second(value):
        return lax.ppermute(value, "section", [(0, 1)])

    def to_second_all(*values):
        return [to_second(v) for v in values]

    def settle(first_layer, first_other, second_layer, second_other):
        return (
            jnp.where(core == 0, first_layer, second_other),
            jnp.where(core == 0, first_other, second_layer),
        )

    def place(first_layer, second_layer):
        return settle(first_layer, to_first(first_layer), second_layer, to_second(second_layer))

    def add_peers(gains):
        return sum((head_peer(gains, k) for k in range(1, peers)), gains)

    def backward(layer, gyb, gfirst, kept, late, before):
        x_own, n1, (query, key_value, o, lse), ob, w_out, fed, w_qkv, w_gate_up, w_down = kept
        hid, r2, n2, gate, up, act = fed
        sigmoid = jax.nn.sigmoid(gate)
        da = dot(gyb, w_down, ((1,), (0,)))
        dgate = da * up * sigmoid * (1.0 + gate * (1.0 - sigmoid))
        dup = da * (gate * sigmoid)
        dgu = jnp.concatenate([dgate, dup], axis=1).astype(BF16)

        def grad_rows(a, b):
            return dot(a, b, ((0,), (0,))).astype(BF16)

        def gain_rows(dn, n, g):
            return jnp.sum(dn.astype(F32) * n.astype(F32), axis=0) / g

        def beside_ffn(dn, n2, dgu):
            g_gate_up, g_gain = grad_rows(n2, dgu), gain_rows(dn, n2, gain[layer, 1])
            if layer:
                return g_gate_up, g_gain
            return g_gate_up, g_gain, to_second(before[2])

        dn2 = dot(dgu, w_gate_up, ((1,), (1,))).astype(BF16)
        dn2, (g_gate_up, g_ffn_gain, *y_other) = reduce_tokens(dn2, beside_ffn, (dn2, n2, dgu))
        c2 = hid * r2
        e2 = dn2 * gain[layer, 1]
        gh = gyb[:part].astype(F32) + r2 * (e2 - c2 * jnp.mean(e2 * c2, axis=-1, keepdims=True))
        ghb, g_gate_up = barrier((gh.astype(BF16), g_gate_up))
        gate_up_rows = scatter_rows(g_gate_up)

        def beside_ghb(gyb, act):
            return (grad_rows(gyb, act), *(() if layer else (to_second(gyb),)))

        ghb, (g_down, *gx_other) = gather_tokens(ghb, beside_ghb, (gyb, act))
        dob = dot(w_out[:, :local], ghb, ((0,), (1,))).astype(BF16)
        dob = dob.reshape(heads, HEAD_DIM, rows)

        def grad_rest(ghb, ob, g_down):
            g_out = dot(ghb, ob, ((0,), (1,))).astype(BF16)
            return jnp.concatenate([g_out, g_down], axis=1)

        if by_head:
            dob, g_rest = to_heads(dob, grad_rest, (ghb, ob, g_down))
            dob = dob[None]
        else:
            g_rest = grad_rest(ghb, ob, g_down)
            dob = dob[:, None]
        if layer:
            dob, (y_part, y_hid) = barrier((dob, late))
            y_own = (y_hid + reduce_tokens(y_part)).astype(BF16)
        dq, dk, dv = attend_grad(scalars, query, key_value, pos_rows, o, dob, lse)
        if layer:
            dq, y_own = barrier((dq, y_own))
        if by_head:
            dq, dk, dv = dq[0], dk[0], dv[0]
        else:
            dq = dq[:, 0]
            dkv = jnp.stack([dk, dv], axis=1).transpose(2, 0, 1, 3, 4).astype(BF16)
            dkv = lax.psum_scatter(dkv, "seq", scatter_dimension=0, tiled=False).astype(F32)
            dk, dv = dkv[:, 0], dkv[:, 1]
        dq = turn_back(dq, back_cos, back_sin).astype(BF16)
        dk = turn_back(dk, back_cos, back_sin).astype(BF16)
        if gfirst is None:
            dv = (0.5 * dv).astype(BF16)
        else:
            dv = (dv + gfirst.astype(F32)).astype(BF16)
        packed = jnp.stack([dq, dk, dv], axis=1)

        def beside_packed(*values):
            return gather_tokens(*values)[0] if layer else to_second_all(*values)

        values = (y_own,) if layer else before[0]
        if by_head:
            packed, moved = to_tokens(packed, beside_packed, values)
        else:
            moved = beside_packed(*values)
        dqkv = packed.reshape(3 * local, rows)

        dn1 = dot(dqkv, w_qkv, ((0,), (1,))).astype(BF16)
        g_attn_gain = gain_rows(dn1, n1, gain[layer, 0])
        gains = jnp.stack([g_attn_gain, g_ffn_gain])

        def grad_qkv(n1, dqkv):
            g_qkv = dot(n1, dqkv, ((0,), (1,))).astype(BF16)
            return by_rows(jnp.concatenate([g_rest, g_qkv], axis=1))

        dn1, n1, dqkv = barrier((dn1, n1, dqkv))
        g_last = grad_qkv(n1, dqkv)
        if layer:
            dn1 = reduce_tokens(dn1)
        else:
            gains = jnp.concatenate([gains, before[1]], axis=0)
            high = gains.astype(BF16)
            low = (gains - high.astype(F32)).astype(BF16)
            tail = jnp.concatenate([high, low, jnp.zeros((8, width), BF16)], axis=0)
            dn1 = jnp.concatenate([dn1.reshape(peers, part, width)] + [
                jnp.broadcast_to(tail[None], (peers, 16, width))
            ], axis=1).reshape(peers * (part + 16), width)
            dn1 = reduce_tokens(dn1)
            gains = dn1[part : part + 4] + dn1[part + 4 : part + 8]
            dn1 = dn1[:part]
        r1 = lax.rsqrt(jnp.mean(x_own * x_own, axis=-1, keepdims=True) + EPS)
        c1 = x_own * r1
        e1 = dn1 * gain[layer, 0]
        gx = gh + r1 * (e1 - c1 * jnp.mean(e1 * c1, axis=-1, keepdims=True))
        gx = gx.astype(BF16)
        g_last, gate_up_rows = barrier((g_last, gate_up_rows))
        last_rows = scatter_rows(g_last)
        if layer:
            return gather_tokens(gx)[0], dv, (gate_up_rows, last_rows), gains, moved

        def beside_last(gate_up):
            return rows_of(settle(gate_up, to_first(gate_up), before[0][0], moved[0]))

        gx, gate_up = gather_tokens(gx, beside_last, (gate_up_rows,))
        return gx, gate_up, last_rows, gains, y_other[0], gx_other[0], moved[1]

    def rows_of(pair):
        return jnp.concatenate(pair, axis=0).astype(F32)

    def add_devices(gains):
        gains = gains.reshape(2, devices, own)
        mine = lax.dynamic_index_in_dim(gains, seq, 1, keepdims=False)
        for k in range(1, devices):
            block = lax.dynamic_index_in_dim(gains, (seq + k) % devices, 1, keepdims=False)
            mine = mine + seq_shift(block, k)
        return mine

    n1_0, packed, v0 = project(0, x0, w_qkv_first, None)
    ob0, w_out0, attn0, ffn_half = mix(packed, out_first, True, ffn_half)
    gate_up0, down0 = columns(gather_rows(ffn_half), 2 * hidden, hidden)
    ob0, attn_later = barrier((ob0, attn_later))
    attn_later = gather_rows(attn_later)
    y_part, fed0 = feed(0, x0, gather_features(ob0)[0], w_out0, gate_up0, down0)
    y0, _ = gather_tokens((fed0[0] + reduce_tokens(y_part)).astype(BF16))
    qkv1, out1 = columns(attn_later, 3 * local, local)
    out1 = lax.dynamic_index_in_dim(
        out1.reshape(devices, 2, own // 2, local), core, 1, keepdims=False
    )
    n1_1, packed, _ = project(1, y0, qkv1, v0)
    ob1, w_out1, attn1, ffn_later = mix(packed, out1, False, ffn_later)
    gate_up1, down1 = columns(gather_rows(ffn_later), 2 * hidden, hidden)
    ob_all, y0_first = gather_features(ob1, to_first, (y0,))
    y_part, fed1 = feed(1, y0, ob_all, w_out1, gate_up1, down1)
    kept0 = (x0[:part].astype(F32), n1_0, attn0, ob0, w_out0, fed0, w_qkv_first, gate_up0, down0)
    kept1 = (y0[:part].astype(F32), n1_1, attn1, ob1, w_out1, fed1, qkv1, gate_up1, down1)
    gx1, gfirst, rows1, gains1, y1 = backward(1, gy1, None, kept1, (y_part, fed1[0]), ())
    gx0, gate_up_grad, last_rows, gains, y1_second, gx1_second, last_second = backward(
        0, gx1, gfirst, kept0, (), (rows1, gains1, y1)
    )

    def tokens_of(pair, dtype):
        return jnp.stack([peer_order(m).astype(dtype) for m in pair])[None]

    activations = tokens_of(settle(y0, y0_first, y1, y1_second), BF16)
    gx0_first = to_first(gx0)
    input_grads = tokens_of(settle(gx0, gx0_first, gx1, gx1_second), F32)
    gains = gains.reshape(2, 2, width)
    gains = lax.dynamic_index_in_dim(gains, core, 0, keepdims=False) + core_swap(
        lax.dynamic_index_in_dim(gains, 1 - core, 0, keepdims=False)
    )
    gains = add_devices(gains)
    gate_up_grad = gate_up_grad.reshape(1, own, 2, hidden)
    last = rows_of(settle(last_rows, to_first(last_rows), rows1[1], last_second))
    out_grad, down_grad, qkv_grad = columns(last, local, hidden, 3 * local)
    out_grad, down_grad = out_grad[None], down_grad[None]
    qkv_grad = (
        qkv_grad.reshape(1, own, heads, 3, HEAD_DIM)
        .transpose(0, 1, 3, 2, 4)
        .reshape(1, own, 3, local)
    )
    return (
        activations,
        input_grads,
        qkv_grad,
        out_grad,
        gate_up_grad,
        down_grad,
        gains[0][None],
        gains[1][None],
    )


def solution(mesh):
    placed = (
        P(None, "seq", None),
        P(None, "seq"),
        P(None, "seq", None),
        P("section", "seq", None, "head"),
        P("section", "seq", "head"),
        P("section", "seq", None, "head"),
        P("section", "seq", "head"),
        P("section", "seq"),
        P("section", "seq"),
    )
    return jax.shard_map(
        on_device,
        mesh=mesh,
        in_specs=placed,
        out_specs=(
            P("section", None, "seq", None),
            P("section", None, "seq", None),
            P("section", "seq", None, "head"),
            P("section", "seq", "head"),
            P("section", "seq", None, "head"),
            P("section", "seq", "head"),
            P("section", "seq"),
            P("section", "seq"),
        ),
        check_vma=False,
    )
```
